128 devices in a mesh: rng: 8 (over z, y_hi), az: 16 (over y_lo, x, core).
Axes of the slice: x: 4, y: 4 (y_hi: 2, y_lo: 2; y = y_hi * 2 + y_lo), z: 4, core: 2. Of those that a mesh axis runs over, the one named last changes fastest.
Arguments:
- raw_swath: bfloat16 [8192, 2, 16384], P('rng', None, 'az'), may hold values from -6 to 6
- azimuth_filter: bfloat16 [8192, 2, 16384], P(('rng', 'az')), may hold values from -4 to 4
- anchors: int32 [8, 63, 2], replicated, may hold values from 0 to 15872, as said below
- owners: int32 [8, 63], replicated, may hold values from 0 to 15, as said below
- look_bands: int32 [8, 63, 3], replicated, may hold values from 0 to 384
Outputs:
- cross_spectra: float32 [8, 64, 2, 512, 128], P('rng', 'az')
The draws below stay inside these ranges and needn't reach their ends.
Inputs may be any that keep to these rules, and one draw needn't show every extreme that they name: anchors[r, i] is the first line and the first column (in units of 64 cells) of imagette i in strip r; the column is below 16, and below 9 in the last strip; some imagette of each strip starts at line 16384 - 512. `owners`: in each strip every owner appears at most 4 times, and all but one owner exactly 4 times.
All inputs are finite; a program needn't handle non-finite values.
Results may differ from the reference program's by a relative error of at most 0.004.
Values may be sent and summed in bfloat16 or wider, within the bound.
No kernel may reach another device: no remote copies, remote signals or barrier semaphores. Data moves between devices by JAX's collectives and lax.ppermute only.
A program may use at most 128 MiB of HBM per device.

```python
import math
import jax
import jax.numpy as jnp
from jax import lax

AZ_OUTER = 128
AZ_INNER = 128
LINES = 16384
IMG_C = 512
IMG_L = 512
LOOK = 128
COL = 64
CELLS = 8192
IMG_DEV = 4
IMG_STRIP = 63
N_RNG = 8
N_AZ = 16


def draw_anchors(key, part):
    keys = jax.random.split(jax.random.fold_in(key, 23), 4)
    items = jnp.arange(IMG_STRIP, dtype=jnp.int32)[None, :]
    lines = jax.random.randint(keys[0], (N_RNG, IMG_STRIP), 0, LINES - IMG_L + 1, dtype=jnp.int32)
    pick = jax.random.randint(keys[1], (N_RNG, 1), 0, IMG_STRIP, dtype=jnp.int32)
    lines = jnp.where(items == pick, LINES - IMG_L, lines)
    strips = jnp.arange(N_RNG, dtype=jnp.int32)[:, None]
    upper = jnp.where(strips == N_RNG - 1, N_AZ - 7, N_AZ).astype(jnp.int32)
    columns = jax.random.randint(keys[2], (N_RNG, IMG_STRIP), 0, upper, dtype=jnp.int32)
    pick_column = jax.random.randint(keys[3], (N_RNG, 1), 0, IMG_STRIP, dtype=jnp.int32)
    columns = jnp.where(items == pick_column, upper - 1, columns)
    return jnp.stack([lines, columns], axis=-1).astype(jnp.int32)


def draw_owners(key, part):
    keys = jax.random.split(jax.random.fold_in(key, 11), N_RNG)

    def one_strip(strip_key):
        slots = jax.random.permutation(strip_key, N_AZ * IMG_DEV)[:IMG_STRIP]
        return (slots // IMG_DEV).astype(jnp.int32)
    return jax.vmap(one_strip)(keys)


def draw_look_bands(key, part):
    keys = jax.random.split(jax.random.fold_in(key, 37), 2)
    starts = jax.random.randint(keys[0], (N_RNG, IMG_STRIP, 3), 0, IMG_L - LOOK + 1, dtype=jnp.int32)
    pick = jax.random.randint(keys[1], (N_RNG, 1, 1), 0, IMG_STRIP, dtype=jnp.int32)
    items = jnp.arange(IMG_STRIP, dtype=jnp.int32)[None, :, None]
    looks = jnp.arange(3, dtype=jnp.int32)[None, None, :]
    return jnp.where((items == pick) & (looks == 1), IMG_L - LOOK, starts).astype(jnp.int32)


def shard_levels(own_key, dims, cuts, low, largest):
    gain = 1.0
    for axis_at, blocks in cuts:
        heights = jax.random.uniform(jax.random.fold_in(jax.random.fold_in(own_key, 6), axis_at), (blocks,), jnp.float32, low / len(cuts), largest / len(cuts))
        gain = gain * jnp.repeat(jnp.exp(heights), dims[axis_at] // blocks).reshape((-1,) + (1,) * (len(dims) - 1 - axis_at))
    return gain


def scatter_about(rng, shape, spread, limit, shards=(), kind=jnp.bfloat16):
    entries = jax.random.normal(rng, shape, jnp.float32) * spread
    if len(shards) > 0:
        entries = shard_levels(rng, shape, shards, -0.22, 0.18) * entries
    return jnp.clip(entries, min=-limit, max=limit).astype(kind)


def setup_inputs(seed: int = 0) -> dict:
    key_of = jax.random.split(jax.random.key(seed), 6)
    return {
        "raw_swath": scatter_about(key_of[0], (CELLS, 2, LINES), 1.0, 6.0, ((0, 8), (2, 16))),
        "azimuth_filter": scatter_about(key_of[1], (CELLS, 2, LINES), 0.7, 4.0, ((0, 128),)),
        "anchors": draw_anchors(jax.random.fold_in(key_of[5], 71), 0),
        "owners": draw_owners(jax.random.fold_in(key_of[5], 71), 0),
        "look_bands": draw_look_bands(jax.random.fold_in(key_of[5], 71), 0),
    }


full_turn = 2.0 * math.pi
epsilon = 1e-06

def dft_table(length, sign):
    steps = jnp.arange(length, dtype=jnp.int32)
    phase = steps[:, None] * steps[None, :] % length
    angle = full_turn * phase.astype(jnp.float32) / length
    scale = 1.0 / math.sqrt(length)
    return ((jnp.cos(angle) * scale).astype(jnp.bfloat16), (sign * jnp.sin(angle) * scale).astype(jnp.bfloat16))

def twiddle_table(sign):
    outer = jnp.arange(AZ_OUTER, dtype=jnp.int32)
    inner = jnp.arange(AZ_INNER, dtype=jnp.int32)
    phase = outer[:, None] * inner[None, :] % (AZ_OUTER * AZ_INNER)
    angle = full_turn * phase.astype(jnp.float32) / (AZ_OUTER * AZ_INNER)
    return (jnp.cos(angle), sign * jnp.sin(angle))

def mix(form, left, right):
    return jnp.einsum(form, left.astype(jnp.float32), right.astype(jnp.float32))

def complex_sum(form, left_re, left_im, right_re, right_im):
    out_re = mix(form, left_re, right_re) - mix(form, left_im, right_im)
    out_im = mix(form, left_re, right_im) + mix(form, left_im, right_re)
    return (out_re, out_im)

def focus_lines(turned, response):
    count = turned.shape[0]
    lines_re = turned[:, 0].reshape(count, AZ_OUTER, AZ_INNER)
    lines_im = turned[:, 1].reshape(count, AZ_OUTER, AZ_INNER)
    outer_re, outer_im = dft_table(AZ_OUTER, -1.0)
    inner_re, inner_im = dft_table(AZ_INNER, -1.0)
    twist_re, twist_im = twiddle_table(-1.0)
    first_re, first_im = complex_sum('cab,ak->ckb', lines_re, lines_im, outer_re, outer_im)
    section_re = (first_re * twist_re - first_im * twist_im).astype(jnp.bfloat16)
    section_im = (first_re * twist_im + first_im * twist_re).astype(jnp.bfloat16)
    second_re, second_im = complex_sum('ckb,bm->ckm', section_re, section_im, inner_re, inner_im)
    gain_re = response[:, 0].reshape(count, AZ_OUTER, AZ_INNER).astype(jnp.float32)
    gain_im = response[:, 1].reshape(count, AZ_OUTER, AZ_INNER).astype(jnp.float32)
    shaped_re = (second_re * gain_re - second_im * gain_im).astype(jnp.bfloat16)
    shaped_im = (second_re * gain_im + second_im * gain_re).astype(jnp.bfloat16)
    back_outer_re, back_outer_im = dft_table(AZ_OUTER, 1.0)
    back_inner_re, back_inner_im = dft_table(AZ_INNER, 1.0)
    untwist_re, untwist_im = twiddle_table(1.0)
    third_re, third_im = complex_sum('ckm,mb->ckb', shaped_re, shaped_im, back_inner_re, back_inner_im)
    rest_re = (third_re * untwist_re - third_im * untwist_im).astype(jnp.bfloat16)
    rest_im = (third_re * untwist_im + third_im * untwist_re).astype(jnp.bfloat16)
    final_re, final_im = complex_sum('ckb,ka->cab', rest_re, rest_im, back_outer_re, back_outer_im)
    return jnp.stack([final_re.reshape(count, -1), final_im.reshape(count, -1)], axis=1).astype(jnp.bfloat16)

def azimuth_spectrum(image):
    table_re, table_im = dft_table(IMG_L, -1.0)
    out_re, out_im = complex_sum('...cn,nf->...cf', image[..., 0, :], image[..., 1, :], table_re, table_im)
    return jnp.stack([out_re, out_im], axis=-2).astype(jnp.bfloat16)

def cross_spectrum(spectrum, starts):
    back_re, back_im = dft_table(LOOK, 1.0)
    ahead_re, ahead_im = dft_table(LOOK, -1.0)
    across_re_tab, across_im_tab = dft_table(IMG_C, -1.0)
    waves = []
    for number in range(3):
        band = lax.dynamic_slice_in_dim(spectrum, starts[number], LOOK, 2)
        look_re, look_im = complex_sum('cf,fm->cm', band[:, 0], band[:, 1], back_re, back_im)
        power = look_re * look_re + look_im * look_im
        contrast = (power / (jnp.mean(power) + epsilon) - 1.0).astype(jnp.bfloat16)
        across_re = mix('pc,cm->pm', across_re_tab, contrast).astype(jnp.bfloat16)
        across_im = mix('pc,cm->pm', across_im_tab, contrast).astype(jnp.bfloat16)
        waves.append(complex_sum('pm,mv->pv', across_re, across_im, ahead_re, ahead_im))
    total_re = jnp.zeros((IMG_C, LOOK), jnp.float32)
    total_im = jnp.zeros((IMG_C, LOOK), jnp.float32)
    for first, second in ((0, 1), (1, 2), (0, 2)):
        one_re, one_im = waves[first]
        two_re, two_im = waves[second]
        total_re = total_re + one_re * two_re + one_im * two_im
        total_im = total_im + one_im * two_re - one_re * two_im
    return jnp.stack([total_re, total_im])

def slot_table(owner_row, azimuth_count, capacity):
    labels = jnp.arange(azimuth_count, dtype=jnp.int32)
    owners_hot = (owner_row[:, None] == labels[None, :]).astype(jnp.int32)
    earlier = jnp.cumsum(owners_hot, axis=0) - owners_hot
    rank = lax.optimization_barrier(jnp.sum(earlier * owners_hot, axis=1))
    match = (owner_row[None, None, :] == labels[:, None, None]) & (rank[None, None, :] == jnp.arange(capacity, dtype=jnp.int32)[None, :, None])
    filled = jnp.any(match, axis=2)
    items = jnp.arange(owner_row.shape[0], dtype=jnp.int32)
    chosen = lax.optimization_barrier(jnp.sum(jnp.where(match, items[None, None, :], 0), axis=2)).astype(jnp.int32)
    return (filled, chosen)

def reference(raw_swath, azimuth_filter, anchors, owners, look_bands):
    cells = raw_swath.shape[0]
    strip_cells = cells // N_RNG
    focused = lax.map(lambda pair: focus_lines(pair[0], pair[1]), (raw_swath.reshape(N_RNG, strip_cells, 2, LINES), azimuth_filter.reshape(N_RNG, strip_cells, 2, LINES))).reshape(cells, 2, LINES)
    filled, chosen = jax.vmap(lambda row: slot_table(row, N_AZ, IMG_DEV))(owners)
    strip_ids = jnp.arange(N_RNG, dtype=jnp.int32)[:, None, None]
    start_lines = anchors[strip_ids, chosen, 0].astype(jnp.int32)
    start_cells = (strip_ids * strip_cells + anchors[strip_ids, chosen, 1] * COL).astype(jnp.int32)
    slot_bands = look_bands[strip_ids, chosen].astype(jnp.int32)

    def one_slot(item):
        first_cell, first_line, starts = item
        image = lax.dynamic_slice(focused, (first_cell, jnp.zeros((), jnp.int32), first_line), (IMG_C, 2, IMG_L))
        return cross_spectrum(azimuth_spectrum(image), starts)
    results = lax.map(one_slot, (start_cells.reshape(-1), start_lines.reshape(-1), slot_bands.reshape(-1, 3)))
    results = jnp.where(filled.reshape(-1)[:, None, None, None], results, jnp.zeros_like(results))
    return results.reshape(N_RNG, N_AZ * IMG_DEV, 2, IMG_C, LOOK)
```

```python
import math

import jax
import jax.numpy as jnp
import numpy as np
from jax import lax
from jax.experimental import pallas as pl
from jax.experimental.pallas import tpu as pltpu
from jax.sharding import PartitionSpec as P

AZ_OUTER = 128
AZ_INNER = 128
LINES = 16384
IMG_C = 512
IMG_L = 512
LOOK = 128
COL = 64
IMG_DEV = 4
SPAN = IMG_C // COL
BLOCK = 8
TURN_ROWS = 16
epsilon = 1e-06
bf16 = jnp.bfloat16
f32 = jnp.float32


def dft_np(length, sign):
    steps = np.arange(length)
    phase = (steps[:, None] * steps[None, :]) % length
    angle = 2.0 * math.pi * phase / length
    scale = 1.0 / math.sqrt(length)
    return np.cos(angle) * scale, sign * np.sin(angle) * scale


def low(table):
    return np.asarray(table, np.float32).astype(jnp.bfloat16)


def left_form(length, sign):
    re, im = dft_np(length, sign)
    return low(np.block([[re, -im], [im, re]]))


def right_form(length, sign):
    re, im = dft_np(length, sign)
    return low(np.block([[re, im], [-im, re]]))


def twiddles():
    steps = np.arange(AZ_OUTER)
    angle = 2.0 * math.pi * ((steps[:, None] * steps[None, :]) % LINES) / LINES
    return np.stack([np.cos(angle), -np.sin(angle)]).astype(np.float32)


def dot(left, right):
    return jnp.dot(left, right, preferred_element_type=f32)


def focus_kernel(arr_ref, filt_ref, l1_ref, t2_ref, t3_ref, l4_ref, tw_ref, x_ref, y_ref, *, steps):
    step = pl.program_id(0)

    @pl.when(step < steps)
    def _():
        tw_re = tw_ref[0]
        tw_im = tw_ref[1]
        for pair in range(BLOCK // 2):
            cells = (2 * pair, 2 * pair + 1)

            def stacked(cell):
                return jnp.concatenate(
                    [arr_ref[:, cell, part].reshape(AZ_OUTER, AZ_INNER) for part in (0, 1)], axis=0
                )

            out = dot(l1_ref[...], jnp.concatenate([stacked(c) for c in cells], axis=1))
            rows = []
            for half in (0, 1):
                re = out[:128, half * 128 : half * 128 + 128]
                im = out[128:, half * 128 : half * 128 + 128]
                rows.append(
                    jnp.concatenate([re * tw_re - im * tw_im, re * tw_im + im * tw_re], axis=1)
                )
            section = jnp.concatenate(rows, axis=0).astype(bf16)
            out = dot(section, t2_ref[...])
            rows = []
            for half in (0, 1):
                re = out[half * 128 : half * 128 + 128, :128]
                im = out[half * 128 : half * 128 + 128, 128:]
                g_re = filt_ref[cells[half], 0].astype(f32)
                g_im = filt_ref[cells[half], 1].astype(f32)
                rows.append(jnp.concatenate([re * g_re - im * g_im, re * g_im + im * g_re], axis=1))
            spectrum = jnp.concatenate(rows, axis=0).astype(bf16)
            out = dot(spectrum, t3_ref[...])
            columns = []
            for half in (0, 1):
                re = out[half * 128 : half * 128 + 128, :128]
                im = out[half * 128 : half * 128 + 128, 128:]
                columns.append(
                    jnp.concatenate([re * tw_re + im * tw_im, im * tw_re - re * tw_im], axis=0)
                )
            out = dot(l4_ref[...], jnp.concatenate(columns, axis=1).astype(bf16))
            for half in (0, 1):
                cell = step * BLOCK + cells[half]
                y_ref[pl.ds(cell * 128, 128), :] = out[:128, half * 128 : half * 128 + 128]
                y_ref[pl.ds((COL + cell) * 128, 128), :] = out[128:, half * 128 : half * 128 + 128]

    @pl.when(step >= steps)
    def _():
        first = (step - steps) * TURN_ROWS
        for row in range(TURN_ROWS):
            block = y_ref[pl.ds(first + row, 128, stride=128), :]
            x_ref[row * 128 : row * 128 + 128, :] = block.T.astype(bf16)


def focus(arrived, response):
    steps = COL // BLOCK
    turns = AZ_OUTER // TURN_ROWS
    whole = lambda shape: pl.BlockSpec(shape, lambda i: (0,) * len(shape))
    return pl.pallas_call(
        lambda *refs: focus_kernel(*refs, steps=steps),
        out_shape=jax.ShapeDtypeStruct((LINES, 2 * COL), bf16),
        grid=(steps + turns,),
        in_specs=[
            pl.BlockSpec((16, BLOCK, 2, 8, 128), lambda i: (0, jnp.minimum(i, steps - 1), 0, 0, 0)),
            pl.BlockSpec((BLOCK, 2, 128, 128), lambda i: (jnp.minimum(i, steps - 1), 0, 0, 0)),
            whole((256, 256)),
            whole((256, 256)),
            whole((256, 256)),
            whole((256, 256)),
            whole((2, 128, 128)),
        ],
        out_specs=pl.BlockSpec((TURN_ROWS * 128, 128), lambda i: (jnp.maximum(i - steps, 0), 0)),
        scratch_shapes=[pltpu.VMEM((LINES, 128), f32)],
        name="focus",
    )(
        arrived,
        response,
        jnp.asarray(left_form(128, -1.0)),
        jnp.asarray(right_form(128, -1.0)),
        jnp.asarray(right_form(128, 1.0)),
        jnp.asarray(left_form(128, 1.0)),
        jnp.asarray(twiddles()),
    )


def turned(value, sign):
    return pltpu.roll(value, 64, 1) * sign


def powers_kernel(info_ref, *refs, resumed):
    if resumed:
        x_ref, w_ref, u_ref, old_ref, out_ref, lines_ref, spec_ref = refs
    else:
        x_ref, w_ref, u_ref, out_ref, lines_ref, spec_ref = refs
        old_ref = None
    owner = pl.program_id(0)
    lane = lax.broadcasted_iota(jnp.int32, (1, 128), 1)
    sign = jnp.where(lane < 64, -1.0, 1.0).astype(f32)

    @pl.when(owner == 0)
    def _():
        def widen(part, carry):
            rows = pl.ds(pl.multiple_of(part * 1024, 1024), 1024)
            lines_ref[rows, :] = x_ref[rows, :].astype(f32)
            return carry

        lax.fori_loop(0, LINES // 1024, widen, 0)

    for pair in range(2):
        slots = [owner * IMG_DEV + 2 * pair + half for half in (0, 1)]
        keeps = [info_ref[slot * 8 + 1] for slot in slots]

        if resumed:
            out_ref[0, pair] = old_ref[0, pair]

        @pl.when(keeps[0] + keeps[1] > 0)
        def _():
            columns = []
            for slot in slots:
                image = lines_ref[pl.ds(info_ref[slot * 8], IMG_L), :]
                columns.append(
                    jnp.concatenate([image.astype(bf16), turned(image, sign).astype(bf16)], axis=0)
                )
            spectra = dot(w_ref[...], jnp.concatenate(columns, axis=1))
            for half in (0, 1):
                spec_ref[half * IMG_L : half * IMG_L + IMG_L, :] = spectra[:, half * 128 : half * 128 + 128]
            for look in range(3):
                powers = []
                for half, slot in enumerate(slots):
                    band = spec_ref[pl.ds(half * IMG_L + info_ref[slot * 8 + 2 + look], LOOK), :]
                    both = jnp.concatenate([band.astype(bf16), turned(band, sign).astype(bf16)], axis=0)
                    value = dot(u_ref[...], both)
                    square = value * value
                    powers.append(square + pltpu.roll(square, 64, 1))
                power = jnp.where(lane < 64, powers[0], powers[1]).astype(bf16)
                if resumed:
                    fresh = jnp.where(lane < 64, keeps[0], keeps[1]) > 0
                    power = jnp.where(fresh, power.astype(f32), old_ref[0, pair, look].astype(f32)).astype(bf16)
                out_ref[0, pair, look] = power


def looks_of(info, lines, old=None):
    re, im = dft_np(IMG_L, -1.0)
    back_re, back_im = dft_np(LOOK, 1.0)
    whole = lambda shape: pl.BlockSpec(shape, lambda i, s: (0,) * len(shape))
    block = pl.BlockSpec((1, 2, 3, 128, 128), lambda i, s: (i, 0, 0, 0, 0))
    resumed = old is not None
    owners = 16
    return pl.pallas_call(
        lambda *refs: powers_kernel(*refs, resumed=resumed),
        out_shape=jax.ShapeDtypeStruct((owners, 2, 3, 128, 128), bf16),
        grid_spec=pltpu.PrefetchScalarGridSpec(
            num_scalar_prefetch=1,
            grid=(owners,),
            in_specs=[whole((LINES, 128)), whole((IMG_L, 2 * IMG_L)), whole((LOOK, 2 * LOOK))]
            + ([block] if resumed else []),
            out_specs=block,
            scratch_shapes=[pltpu.VMEM((LINES, 128), f32), pltpu.VMEM((2 * IMG_L, 128), f32)],
        ),
        name="looks_beyond" if resumed else "looks_own",
    )(
        info,
        lines,
        jnp.asarray(low(np.concatenate([re, im], axis=1))),
        jnp.asarray(low(np.concatenate([back_re, back_im], axis=1))),
        *([old] if resumed else []),
    )


def cross_kernel(info_ref, arr_ref, w_ref, l_ref, out_ref):
    pair = pl.program_id(0)
    lane = lax.broadcasted_iota(jnp.int32, (1, 128), 1)
    for half in (0, 1):
        slot = 2 * pair + half
        start = info_ref[slot * 2]
        filled = info_ref[slot * 2 + 1] > 0
        rows = []
        for look in range(3):
            pieces = []
            for part in range(SPAN // 2):
                ahead = arr_ref[(start + 2 * part) % 16, 0, look].astype(f32)
                after = arr_ref[(start + 2 * part + 1) % 16, 0, look].astype(f32)
                if half == 0:
                    after = pltpu.roll(after, 64, 1)
                else:
                    ahead = pltpu.roll(ahead, 64, 1)
                pieces.append(jnp.where(lane < 64, ahead, after))
            power = jnp.concatenate(pieces, axis=1)
            mean = jnp.sum(power) * (1.0 / (IMG_C * LOOK))
            rows.append((power / (mean + epsilon) - 1.0).astype(bf16))
        across = dot(jnp.concatenate(rows, axis=0), w_ref[...]).astype(bf16)
        waves = []
        for look in range(3):
            part = across[look * 128 : look * 128 + 128]
            both = jnp.concatenate([part[:, :IMG_C], part[:, IMG_C:]], axis=0)
            value = dot(l_ref[...], both)
            waves.append((value[:128], value[128:]))
        total_re = jnp.zeros((LOOK, IMG_C), f32)
        total_im = jnp.zeros((LOOK, IMG_C), f32)
        for first, second in ((0, 1), (1, 2), (0, 2)):
            one_re, one_im = waves[first]
            two_re, two_im = waves[second]
            total_re = total_re + one_re * two_re + one_im * two_im
            total_im = total_im + one_im * two_re - one_re * two_im
        out_ref[half, 0] = jnp.where(filled, total_re, 0.0).T
        out_ref[half, 1] = jnp.where(filled, total_im, 0.0).T


def cross(info, arrived):
    re, im = dft_np(IMG_C, -1.0)
    whole = lambda shape: pl.BlockSpec(shape, lambda i, s: (0,) * len(shape))
    return pl.pallas_call(
        cross_kernel,
        out_shape=jax.ShapeDtypeStruct((IMG_DEV, 2, IMG_C, LOOK), f32),
        grid_spec=pltpu.PrefetchScalarGridSpec(
            num_scalar_prefetch=1,
            grid=(2,),
            in_specs=[
                pl.BlockSpec((16, 1, 3, 128, 128), lambda i, s: (0, i, 0, 0, 0)),
                whole((IMG_C, 2 * IMG_C)),
                whole((256, 256)),
            ],
            out_specs=pl.BlockSpec((2, 2, IMG_C, LOOK), lambda i, s: (i, 0, 0, 0)),
        ),
        name="cross",
    )(info, arrived, jnp.asarray(low(np.concatenate([re, im], axis=1))), jnp.asarray(left_form(128, -1.0)))


def slot_info(anchors, owners, look_bands, strip, column, count):
    row = lax.dynamic_index_in_dim(owners, strip, 0, keepdims=False)
    facts = jnp.concatenate(
        [
            lax.dynamic_index_in_dim(anchors, strip, 0, keepdims=False),
            lax.dynamic_index_in_dim(look_bands, strip, 0, keepdims=False),
        ],
        axis=1,
    )
    items = jnp.arange(row.shape[0], dtype=jnp.int32)
    earlier = (row[:, None] == row[None, :]) & (items[None, :] < items[:, None])
    rank = jnp.sum(earlier.astype(jnp.int32), axis=1)
    place = row * IMG_DEV + rank
    slots = jnp.arange(count * IMG_DEV, dtype=jnp.int32)
    hot = (place[None, :] == slots[:, None]).astype(jnp.int32)
    filled = jnp.sum(hot, axis=1)
    chosen = jnp.sum(hot[:, :, None] * facts[None], axis=1)
    line = jnp.clip(chosen[:, 0], 0, LINES - IMG_L)
    start = chosen[:, 1]
    bands = jnp.clip(chosen[:, 2:], 0, IMG_L - LOOK)
    own = (start <= column) & (column < start + SPAN) & (filled > 0)
    shifted = column + count
    beyond = (start <= shifted) & (shifted < start + SPAN) & (filled > 0)
    pad = jnp.zeros((slots.shape[0], 3), jnp.int32)

    def listed(keep):
        return jnp.concatenate(
            [line[:, None], keep.astype(jnp.int32)[:, None], bands, pad], axis=1
        ).reshape(-1)

    mine = jnp.stack([start, filled], axis=1)
    mine = lax.dynamic_slice_in_dim(mine, column * IMG_DEV, IMG_DEV, 0).reshape(-1)
    return listed(own), listed(beyond), mine


def shards(raw_swath, azimuth_filter, anchors, owners, look_bands):
    count = lax.axis_size("az")
    strips = lax.axis_size("rng")
    strip = lax.axis_index("rng")
    column = lax.axis_index("az")
    own, beyond, mine = slot_info(anchors, owners, look_bands, strip, column, count)
    pieces = raw_swath.reshape(count, COL, 2, 8, 128)
    arrived = lax.all_to_all(pieces, "az", split_axis=0, concat_axis=0, tiled=True)
    lines = focus(arrived, azimuth_filter.reshape(COL, 2, AZ_OUTER, AZ_INNER))
    reach = [
        ((r + 1) * count + c, r * count + c) for r in range(strips - 1) for c in range(SPAN - 1)
    ]
    next_lines = lax.ppermute(lines, ("rng", "az"), reach)
    powers = looks_of(own, lines)
    powers = looks_of(beyond, next_lines, powers)
    powers = lax.all_to_all(powers, "az", split_axis=0, concat_axis=0, tiled=True)
    return cross(mine, powers)[None]


def solution(mesh):
    in_specs = (P("rng", None, "az"), P(("rng", "az"), None, None), P(), P(), P())
    out_specs = P("rng", "az", None, None, None)
    return jax.shard_map(shards, mesh=mesh, in_specs=in_specs, out_specs=out_specs, check_vma=False)
```

```python
import math

import jax
import jax.numpy as jnp
import numpy as np
from jax import lax
from jax.experimental import pallas as pl
from jax.experimental.pallas import tpu as pltpu
from jax.sharding import PartitionSpec as P


AZ_OUTER = 128
AZ_INNER = 128
LINES = 16384
IMG_C = 512
IMG_L = 512
LOOK = 128
COL = 64
IMG_DEV = 4
SPAN = IMG_C // COL
BLOCK = 8
TURN_ROWS = 16
MERGED = 4
epsilon = 1e-06
bf16 = jnp.bfloat16
f32 = jnp.float32


def dft_np(length, sign):
    steps = np.arange(length)
    phase = (steps[:, None] * steps[None, :]) % length
    angle = 2.0 * math.pi * phase / length
    scale = 1.0 / math.sqrt(length)
    return np.cos(angle) * scale, sign * np.sin(angle) * scale


def low(table):
    return np.asarray(table, np.float32).astype(jnp.bfloat16)


def left_form(length, sign):
    re, im = dft_np(length, sign)
    return low(np.block([[re, -im], [im, re]]))


def right_form(length, sign):
    re, im = dft_np(length, sign)
    return low(np.block([[re, im], [-im, re]]))


def twiddles():
    steps = np.arange(AZ_OUTER)
    angle = 2.0 * math.pi * ((steps[:, None] * steps[None, :]) % LINES) / LINES
    return np.stack([np.cos(angle), -np.sin(angle)]).astype(np.float32)


def dot(left, right):
    return jnp.dot(left, right, preferred_element_type=f32)


def focus_kernel(arr_ref, filt_ref, l1_ref, t2_ref, t3_ref, l4_ref, tw_ref, x_ref, y_ref, *, steps):
    step = pl.program_id(0)

    @pl.when(step < steps)
    def _():
        tw_re = tw_ref[0]
        tw_im = tw_ref[1]
        for pair in range(BLOCK // 2):
            cells = (2 * pair, 2 * pair + 1)

            def stacked(cell):
                return jnp.concatenate(
                    [arr_ref[:, cell, part].reshape(AZ_OUTER, AZ_INNER) for part in (0, 1)], axis=0
                )

            out = dot(l1_ref[...], jnp.concatenate([stacked(c) for c in cells], axis=1))
            rows = []
            for half in (0, 1):
                re = out[:128, half * 128 : half * 128 + 128]
                im = out[128:, half * 128 : half * 128 + 128]
                rows.append(
                    jnp.concatenate([re * tw_re - im * tw_im, re * tw_im + im * tw_re], axis=1)
                )
            section = jnp.concatenate(rows, axis=0).astype(bf16)
            out = dot(section, t2_ref[...])
            rows = []
            for half in (0, 1):
                re = out[half * 128 : half * 128 + 128, :128]
                im = out[half * 128 : half * 128 + 128, 128:]
                g_re = filt_ref[cells[half], 0].astype(f32)
                g_im = filt_ref[cells[half], 1].astype(f32)
                rows.append(jnp.concatenate([re * g_re - im * g_im, re * g_im + im * g_re], axis=1))
            spectrum = jnp.concatenate(rows, axis=0).astype(bf16)
            out = dot(spectrum, t3_ref[...])
            columns = []
            for half in (0, 1):
                re = out[half * 128 : half * 128 + 128, :128]
                im = out[half * 128 : half * 128 + 128, 128:]
                columns.append(
                    jnp.concatenate([re * tw_re + im * tw_im, im * tw_re - re * tw_im], axis=0)
                )
            out = dot(l4_ref[...], jnp.concatenate(columns, axis=1).astype(bf16))
            for half in (0, 1):
                cell = step * BLOCK + cells[half]
                y_ref[pl.ds(cell * 128, 128), :] = out[:128, half * 128 : half * 128 + 128]
                y_ref[pl.ds((COL + cell) * 128, 128), :] = out[128:, half * 128 : half * 128 + 128]

    @pl.when(step >= steps)
    def _():
        first = (step - steps) * TURN_ROWS
        for row in range(TURN_ROWS):
            block = y_ref[pl.ds(first + row, 128, stride=128), :]
            x_ref[row * 128 : row * 128 + 128, :] = block.T.astype(bf16)


def focus(arrived, response):
    steps = COL // BLOCK
    turns = AZ_OUTER // TURN_ROWS
    whole = lambda shape: pl.BlockSpec(shape, lambda i: (0,) * len(shape))
    return pl.pallas_call(
        lambda *refs: focus_kernel(*refs, steps=steps),
        out_shape=jax.ShapeDtypeStruct((LINES, 2 * COL), bf16),
        grid=(steps + turns,),
        in_specs=[
            pl.BlockSpec((16, BLOCK, 2, 8, 128), lambda i: (0, jnp.minimum(i, steps - 1), 0, 0, 0)),
            pl.BlockSpec((BLOCK, 2, 128, 128), lambda i: (jnp.minimum(i, steps - 1), 0, 0, 0)),
            whole((256, 256)),
            whole((256, 256)),
            whole((256, 256)),
            whole((256, 256)),
            whole((2, 128, 128)),
        ],
        out_specs=pl.BlockSpec((TURN_ROWS * 128, 128), lambda i: (jnp.maximum(i - steps, 0), 0)),
        scratch_shapes=[pltpu.VMEM((LINES, 128), f32)],
        name="focus",
    )(
        arrived,
        response,
        jnp.asarray(left_form(128, -1.0)),
        jnp.asarray(right_form(128, -1.0)),
        jnp.asarray(right_form(128, 1.0)),
        jnp.asarray(left_form(128, 1.0)),
        jnp.asarray(twiddles()),
    )


def turned(value, sign):
    return pltpu.roll(value, 64, 1) * sign


def looks_kernel(info_ref, x_ref, w_ref, u_ref, *refs, pair, split, skipped):
    refs = refs[skipped:]
    outs = refs[: 2 if split else 1]
    lines_ref, spec_ref, list_ref = refs[len(outs) :]
    owners = 16
    lane = lax.broadcasted_iota(jnp.int32, (1, 128), 1)
    sign = jnp.where(lane < 64, -1.0, 1.0).astype(f32)
    counts = []
    for half in (0, 1):
        for place in range(20):
            list_ref[half * 20 + place] = 0
        found = 0
        for owner in range(owners):
            list_ref[half * 20 + found] = owner
            found = found + info_ref[(owner * IMG_DEV + 2 * pair + half) * 8 + 1]
        counts.append(found)
    trips = (jnp.maximum(counts[0], counts[1]) + 1) // 2

    @pl.when(trips > 0)
    def _():
        def widen(part, carry):
            rows = pl.ds(pl.multiple_of(part * 1024, 1024), 1024)
            lines_ref[rows, :] = x_ref[rows, :].astype(f32)
            return carry

        lax.fori_loop(0, LINES // 1024, widen, 0)

        def trip(at, carry):
            groups = [[(half, list_ref[half * 20 + 2 * at + nth]) for half in (0, 1)] for nth in (0, 1)]
            for nth, group in enumerate(groups):
                columns = []
                for half, owner in group:
                    first = info_ref[(owner * IMG_DEV + 2 * pair + half) * 8]
                    image = lines_ref[pl.ds(first, IMG_L), :]
                    columns.append(
                        jnp.concatenate([image.astype(bf16), turned(image, sign).astype(bf16)], axis=0)
                    )
                spectra = dot(w_ref[...], jnp.concatenate(columns, axis=1))
                for half in (0, 1):
                    top = (2 * nth + half) * IMG_L
                    spec_ref[top : top + IMG_L, :] = spectra[:, half * 128 : half * 128 + 128]
            for nth, group in enumerate(groups):
                for look in range(3):
                    columns = []
                    for half, owner in group:
                        band = info_ref[(owner * IMG_DEV + 2 * pair + half) * 8 + 2 + look]
                        value = spec_ref[pl.ds((2 * nth + half) * IMG_L + band, LOOK), :]
                        columns.append(
                            jnp.concatenate([value.astype(bf16), turned(value, sign).astype(bf16)], axis=0)
                        )
                    value = dot(u_ref[...], jnp.concatenate(columns, axis=1))
                    for half, owner in group:
                        square = value[:, half * 128 : half * 128 + 128]
                        square = square * square
                        power = (square + pltpu.roll(square, 64, 1)).astype(bf16)
                        lanes = slice(half * 64, half * 64 + 64)
                        if split:
                            outs[0][owner, look, :, lanes] = power[:64, lanes]
                            outs[1][owner, look, :, lanes] = power[64:, lanes]
                        else:
                            outs[0][owner, look, :, lanes] = power[:, lanes]
            return carry

        lax.fori_loop(0, trips, trip, 0)


def looks_of(info, lines, pair, split, after=()):
    re, im = dft_np(IMG_L, -1.0)
    back_re, back_im = dft_np(LOOK, 1.0)
    whole = lambda shape: pl.BlockSpec(shape, lambda i, s: (0,) * len(shape))
    owners = 16
    rows = LOOK // 2 if split else LOOK
    shape = (owners, 3, rows, 128)
    return pl.pallas_call(
        lambda *refs: looks_kernel(*refs, pair=pair, split=split, skipped=len(after)),
        out_shape=[jax.ShapeDtypeStruct(shape, bf16)] * (2 if split else 1),
        grid_spec=pltpu.PrefetchScalarGridSpec(
            num_scalar_prefetch=1,
            grid=(1,),
            in_specs=[whole((LINES, 128)), whole((IMG_L, 2 * IMG_L)), whole((LOOK, 2 * LOOK))]
            + [pl.BlockSpec(memory_space=pl.ANY)] * len(after),
            out_specs=[whole(shape)] * (2 if split else 1),
            scratch_shapes=[
                pltpu.VMEM((LINES, 128), f32),
                pltpu.VMEM((4 * IMG_L, 128), f32),
                pltpu.SMEM((40,), jnp.int32),
            ],
        ),
    )(
        info,
        lines,
        jnp.asarray(low(np.concatenate([re, im], axis=1))),
        jnp.asarray(low(np.concatenate([back_re, back_im], axis=1))),
        *after,
    )


def merge_kernel(flag_ref, own_ref, low_ref, high_ref, *refs, pair):
    out_ref = refs[-1]
    step = pl.program_id(0)
    lane = lax.broadcasted_iota(jnp.int32, (1, 1, 128), 2)
    for at in range(MERGED):
        slot = (step * MERGED + at) * IMG_DEV + 2 * pair
        for part, other_ref in enumerate((low_ref, high_ref)):
            rows = slice(part * 64, part * 64 + 64)
            flags = [flag_ref[(slot + half) * 2 + part] for half in (0, 1)]
            taken = jnp.where(lane < 64, flags[0], flags[1]) > 0
            own = own_ref[at, :, rows].astype(f32)
            out_ref[at, :, rows] = jnp.where(taken, other_ref[at].astype(f32), own).astype(bf16)


def merged(flags, own, low_rows, high_rows, pair, after=()):
    block = lambda rows: pl.BlockSpec((MERGED, 3, rows, 128), lambda i, s: (i, 0, 0, 0))
    return pl.pallas_call(
        lambda *refs: merge_kernel(*refs, pair=pair),
        out_shape=jax.ShapeDtypeStruct(own.shape, bf16),
        grid_spec=pltpu.PrefetchScalarGridSpec(
            num_scalar_prefetch=1,
            grid=(16 // MERGED,),
            in_specs=[block(128), block(64), block(64)] + [pl.BlockSpec(memory_space=pl.ANY)] * len(after),
            out_specs=block(128),
        ),
    )(flags, own, low_rows, high_rows, *after)


def cross_kernel(info_ref, arr_ref, w_ref, l_ref, *refs, pair):
    out_ref = refs[-1]
    lane = lax.broadcasted_iota(jnp.int32, (1, 128), 1)
    for half in (0, 1):
        slot = 2 * pair + half
        start = info_ref[slot * 2]
        filled = info_ref[slot * 2 + 1] > 0
        rows = []
        for look in range(3):

            def piece(at):
                column = start + at
                top = arr_ref[column % 16, look, :64]
                bottom = arr_ref[jnp.where(column < 16, column, column - 8), look, 64:]
                return jnp.concatenate([top, bottom], axis=0).astype(f32)

            pieces = []
            for part in range(SPAN // 2):
                ahead = piece(2 * part)
                after = piece(2 * part + 1)
                if half == 0:
                    after = pltpu.roll(after, 64, 1)
                else:
                    ahead = pltpu.roll(ahead, 64, 1)
                pieces.append(jnp.where(lane < 64, ahead, after))
            power = jnp.concatenate(pieces, axis=1)
            mean = jnp.sum(power) * (1.0 / (IMG_C * LOOK))
            rows.append((power / (mean + epsilon) - 1.0).astype(bf16))
        across = dot(jnp.concatenate(rows, axis=0), w_ref[...]).astype(bf16)
        waves = []
        for look in range(3):
            part = across[look * 128 : look * 128 + 128]
            both = jnp.concatenate([part[:, :IMG_C], part[:, IMG_C:]], axis=0)
            value = dot(l_ref[...], both)
            waves.append((value[:128], value[128:]))
        total_re = jnp.zeros((LOOK, IMG_C), f32)
        total_im = jnp.zeros((LOOK, IMG_C), f32)
        for first, second in ((0, 1), (1, 2), (0, 2)):
            one_re, one_im = waves[first]
            two_re, two_im = waves[second]
            total_re = total_re + one_re * two_re + one_im * two_im
            total_im = total_im + one_im * two_re - one_re * two_im
        out_ref[half, 0] = jnp.where(filled, total_re, 0.0).T
        out_ref[half, 1] = jnp.where(filled, total_im, 0.0).T


def cross(info, arrived, pair, earlier=None):
    re, im = dft_np(IMG_C, -1.0)
    whole = lambda shape: pl.BlockSpec(shape, lambda i, s: (0,) * len(shape))
    more = [] if earlier is None else [earlier]
    return pl.pallas_call(
        lambda *refs: cross_kernel(*refs, pair=pair),
        out_shape=jax.ShapeDtypeStruct((IMG_DEV, 2, IMG_C, LOOK), f32),
        grid_spec=pltpu.PrefetchScalarGridSpec(
            num_scalar_prefetch=1,
            grid=(1,),
            in_specs=[
                whole((16, 3, 128, 128)),
                whole((IMG_C, 2 * IMG_C)),
                whole((256, 256)),
            ]
            + [pl.BlockSpec(memory_space=pl.ANY)] * len(more),
            out_specs=pl.BlockSpec((2, 2, IMG_C, LOOK), lambda i, s: (pair, 0, 0, 0)),
        ),
        input_output_aliases={4: 0} if more else {},
    )(
        info,
        arrived,
        jnp.asarray(low(np.concatenate([re, im], axis=1))),
        jnp.asarray(left_form(128, -1.0)),
        *more,
    )


def strip_facts(anchors, owners, look_bands, strip, count):
    row = lax.dynamic_index_in_dim(owners, strip, 0, keepdims=False)
    facts = jnp.concatenate(
        [
            lax.dynamic_index_in_dim(anchors, strip, 0, keepdims=False),
            lax.dynamic_index_in_dim(look_bands, strip, 0, keepdims=False),
        ],
        axis=1,
    )
    items = jnp.arange(row.shape[0], dtype=jnp.int32)
    earlier = (row[:, None] == row[None, :]) & (items[None, :] < items[:, None])
    rank = jnp.sum(earlier.astype(jnp.int32), axis=1)
    place = row * IMG_DEV + rank
    slots = jnp.arange(count * IMG_DEV, dtype=jnp.int32)
    hot = (place[None, :] == slots[:, None]).astype(jnp.int32)
    filled = jnp.sum(hot, axis=1)
    chosen = jnp.sum(hot[:, :, None] * facts[None], axis=1)
    line = jnp.clip(chosen[:, 0], 0, LINES - IMG_L)
    bands = jnp.clip(chosen[:, 2:], 0, IMG_L - LOOK)
    return line, chosen[:, 1], bands, filled


def reaches(start, filled, column):
    return ((start <= column) & (column < start + SPAN) & (filled > 0)).astype(jnp.int32)


def listed(line, bands, keep):
    pad = jnp.zeros((keep.shape[0], 3), jnp.int32)
    return jnp.concatenate([line[:, None], keep[:, None], bands, pad], axis=1).reshape(-1)


def staged(raw_swath, azimuth_filter, anchors, owners, look_bands):
    count = lax.axis_size("az")
    strips = lax.axis_size("rng")
    strip = lax.axis_index("rng")
    column = lax.axis_index("az")
    line, start, bands, filled = strip_facts(anchors, owners, look_bands, strip, count)
    own = listed(line, bands, reaches(start, filled, column))
    flags = jnp.stack(
        [
            reaches(start, filled, column + count),
            reaches(start, filled, column + SPAN) * (column >= SPAN).astype(jnp.int32),
        ],
        axis=1,
    ).reshape(-1)
    mine = jnp.stack([start, filled], axis=1)
    mine = lax.dynamic_slice_in_dim(mine, column * IMG_DEV, IMG_DEV, 0).reshape(-1)
    line, start, bands, filled = strip_facts(
        anchors, owners, look_bands, jnp.maximum(strip - 1, 0), count
    )
    keep = reaches(start, filled, column + count) * (strip > 0).astype(jnp.int32)
    beyond = listed(line, bands, keep)

    pieces = raw_swath.reshape(count, COL, 2, 8, 128)
    arrived = lax.all_to_all(pieces, "az", split_axis=0, concat_axis=0, tiled=True)
    lines = focus(arrived, azimuth_filter.reshape(COL, 2, AZ_OUTER, AZ_INNER))
    reach = [
        [((r + 1) * count + c, r * count + c + shift) for r in range(strips - 1) for c in range(SPAN - 1)]
        for shift in (0, SPAN)
    ]
    passed = []
    after = ()
    for pair in (0, 1):
        parts = looks_of(beyond, lines, pair, True, after)
        after = (parts[0],)
        sent = []
        for way in (0, 1):
            sent.append(lax.ppermute(parts[way], ("rng", "az"), reach[way]))
        passed.append(sent)
    kept = []
    for pair in (0, 1):
        kept += looks_of(own, lines, pair, False, after)
        after = (kept[-1],)
    result = None
    for pair in (0, 1):
        powers = merged(flags, kept[pair], *passed[pair], pair, after)
        powers = lax.all_to_all(powers, "az", split_axis=0, concat_axis=0, tiled=True)
        result = cross(mine, powers, pair, result)
    return result[None]


def solution(mesh):
    in_specs = (P("rng", None, "az"), P(("rng", "az"), None, None), P(), P(), P())
    out_specs = P("rng", "az", None, None, None)
    return jax.shard_map(staged, mesh=mesh, in_specs=in_specs, out_specs=out_specs, check_vma=False)
```

```python
import math

import jax
import jax.numpy as jnp
import numpy as np
from jax import lax
from jax.experimental import pallas as pl
from jax.experimental.pallas import tpu as pltpu
from jax.sharding import PartitionSpec as P


AZ_OUTER = 128
AZ_INNER = 128
LINES = 16384
IMG_C = 512
IMG_L = 512
LOOK = 128
COL = 64
IMG_DEV = 4
SPAN = IMG_C // COL
BLOCK = 16
TURN_ROWS = 32
HALF = COL // 2
DEEP = 2
NEAR = 2
epsilon = 1e-06
bf16 = jnp.bfloat16
f32 = jnp.float32


def dft_np(length, sign):
    steps = np.arange(length)
    phase = (steps[:, None] * steps[None, :]) % length
    angle = 2.0 * math.pi * phase / length
    scale = 1.0 / math.sqrt(length)
    return np.cos(angle) * scale, sign * np.sin(angle) * scale


def low(table):
    return np.asarray(table, np.float32).astype(jnp.bfloat16)


def left_form(length, sign):
    re, im = dft_np(length, sign)
    return low(np.block([[re, -im], [im, re]]))


def right_form(length, sign):
    re, im = dft_np(length, sign)
    return low(np.block([[re, im], [-im, re]]))


def twiddles():
    steps = np.arange(AZ_OUTER)
    angle = 2.0 * math.pi * ((steps[:, None] * steps[None, :]) % LINES) / LINES
    return np.stack([np.cos(angle), -np.sin(angle)]).astype(np.float32)


def in_vmem(*values):
    return [pltpu.with_memory_space_constraint(value, pltpu.VMEM) for value in values]


def dot(left, right):
    return jnp.dot(left, right, preferred_element_type=f32)


def focus_kernel(beyond_ref, own_ref, *refs, steps, turns):
    arr_ref, filt_ref, l1_ref, t2_ref, t3_ref, l4_ref, tw_ref, w_ref, near_ref, far_ref, kept_ref = refs[:11]
    y_ref, lines_ref, list_ref, *spec_refs = refs[11:]
    step = pl.program_id(0)

    @pl.when(step < steps)
    def _():
        tw_re = tw_ref[0]
        tw_im = tw_ref[1]
        pairs = range(BLOCK // 2)

        def stacked(cell):
            return jnp.concatenate(
                [arr_ref[:, cell, part].reshape(AZ_OUTER, AZ_INNER) for part in (0, 1)], axis=0
            )

        sections = []
        for pair in pairs:
            out = dot(l1_ref[...], jnp.concatenate([stacked(2 * pair), stacked(2 * pair + 1)], axis=1))
            rows = []
            for half in (0, 1):
                re = out[:128, half * 128 : half * 128 + 128]
                im = out[128:, half * 128 : half * 128 + 128]
                rows.append(
                    jnp.concatenate([re * tw_re - im * tw_im, re * tw_im + im * tw_re], axis=1).astype(bf16)
                )
            sections.append(jnp.concatenate(rows, axis=0))
        spectra = []
        for pair in pairs:
            out = dot(sections[pair], t2_ref[...])
            rows = []
            for half in (0, 1):
                re = out[half * 128 : half * 128 + 128, :128]
                im = out[half * 128 : half * 128 + 128, 128:]
                g_re = filt_ref[2 * pair + half, 0].astype(f32)
                g_im = filt_ref[2 * pair + half, 1].astype(f32)
                rows.append(
                    jnp.concatenate([re * g_re - im * g_im, re * g_im + im * g_re], axis=1).astype(bf16)
                )
            spectra.append(jnp.concatenate(rows, axis=0))
        rests = []
        for pair in pairs:
            out = dot(spectra[pair], t3_ref[...])
            columns = []
            for half in (0, 1):
                re = out[half * 128 : half * 128 + 128, :128]
                im = out[half * 128 : half * 128 + 128, 128:]
                columns.append(
                    jnp.concatenate([re * tw_re + im * tw_im, im * tw_re - re * tw_im], axis=0).astype(bf16)
                )
            rests.append(jnp.concatenate(columns, axis=1))
        for pair in pairs:
            out = dot(l4_ref[...], rests[pair])
            for half in (0, 1):
                cell = step * BLOCK + 2 * pair + half
                y_ref[pl.ds(cell * 128, 128), :] = out[:128, half * 128 : half * 128 + 128]
                y_ref[pl.ds((HALF + cell) * 128, 128), :] = out[128:, half * 128 : half * 128 + 128]

    @pl.when(step >= steps)
    def _():
        first = (step - steps) * TURN_ROWS
        for row in range(TURN_ROWS):
            block = y_ref[pl.ds(first + row, 2 * HALF, stride=128), :]
            block = jnp.concatenate([block[:HALF], block[:HALF], block[HALF:], block[HALF:]], axis=0)
            value = block.T.astype(bf16).astype(f32)
            lines_ref[pl.ds(pl.multiple_of((first + row) * 128, 128), 128), :] = value

    @pl.when(step == steps + turns - 1)
    def _():
        for info_ref, outs in ((beyond_ref, (near_ref, far_ref)), (own_ref, (kept_ref,))):
            trips = listed_trips(info_ref, list_ref)
            look_trips(trips, info_ref, list_ref, lines_ref, spec_refs, w_ref, l4_ref, outs)


def focus(beyond, own, arrived, response, half):
    steps = HALF // BLOCK
    turns = AZ_OUTER // TURN_ROWS
    whole = lambda shape: pl.BlockSpec(shape, lambda i, *s: (0,) * len(shape))
    shapes = [(16, looks, LOOK, 128) for looks in (NEAR, 3 - NEAR, 3)]
    return pl.pallas_call(
        lambda *refs: focus_kernel(*refs, steps=steps, turns=turns),
        out_shape=[jax.ShapeDtypeStruct(shape, bf16) for shape in shapes],
        grid_spec=pltpu.PrefetchScalarGridSpec(
            num_scalar_prefetch=2,
            grid=(steps + turns,),
            in_specs=[
                pl.BlockSpec((16, BLOCK, 2, 8, 128), lambda i, *s: (0, jnp.minimum(i, steps - 1), 0, 0, 0)),
                pl.BlockSpec(
                    (BLOCK, 2, 128, 128), lambda i, *s: (half * steps + jnp.minimum(i, steps - 1), 0, 0, 0)
                ),
                whole((256, 256)),
                whole((256, 256)),
                whole((256, 256)),
                whole((256, 256)),
                whole((2, 128, 128)),
                whole((IMG_L, 2 * IMG_L)),
            ],
            out_specs=[whole(shape) for shape in shapes],
            scratch_shapes=[
                pltpu.VMEM((2 * HALF * 128, 128), f32),
                pltpu.VMEM((LINES, 128), f32),
                pltpu.SMEM((IMG_DEV * (16 + 2 * DEEP),), jnp.int32),
            ]
            + [pltpu.VMEM((2 * IMG_L, 128), f32)] * DEEP,
        ),
    )(
        beyond,
        own,
        arrived,
        response,
        jnp.asarray(left_form(128, -1.0)),
        jnp.asarray(right_form(128, -1.0)),
        jnp.asarray(right_form(128, 1.0)),
        jnp.asarray(left_form(128, 1.0)),
        jnp.asarray(twiddles()),
        window_table(),
    )


def listed_trips(info_ref, list_ref):
    owners = 16
    room = owners + 2 * DEEP
    most = 0
    for slot in range(IMG_DEV):
        for place in range(room):
            list_ref[slot * room + place] = 0
        found = 0
        for owner in range(owners):
            list_ref[slot * room + found] = owner
            found = found + info_ref[(owner * IMG_DEV + slot) * 8 + 1]
        most = jnp.maximum(most, found)
    return (most + DEEP - 1) // DEEP


def look_trips(trips, info_ref, list_ref, lines_ref, spec_refs, w_ref, u_ref, outs):
    room = 16 + 2 * DEEP
    lane = lax.broadcasted_iota(jnp.int32, (1, 128), 1)
    low_lanes = lane < 64
    sign = jnp.where(low_lanes, 1.0, -1.0).astype(f32)
    even = lane % 64 < 32
    split = len(outs) > 1

    def chosen(tiles):
        return jnp.where(low_lanes, jnp.where(even, tiles[0], tiles[1]), jnp.where(even, tiles[2], tiles[3]))

    def trip(at, carry):
        picks = [
            [list_ref[slot * room + DEEP * at + nth] for slot in range(IMG_DEV)] for nth in range(DEEP)
        ]
        places = [[(owner * IMG_DEV + slot) * 8 for slot, owner in enumerate(row)] for row in picks]
        for nth in range(DEEP):
            images = [lines_ref[pl.ds(info_ref[place], IMG_L), :] for place in places[nth]]
            near = jnp.where(even, images[0], images[1])
            far = jnp.where(even, images[2], images[3])
            side = pltpu.roll(jnp.where(low_lanes, far, near), 64, 1) * sign
            main = jnp.where(low_lanes, near, far).astype(bf16)
            right = jnp.concatenate(
                [
                    jnp.concatenate([main, side.astype(bf16)], axis=1),
                    jnp.concatenate([(-side).astype(bf16), main], axis=1),
                ],
                axis=0,
            )
            spectra = dot(w_ref[...], right)
            spec_refs[nth][:IMG_L, :] = spectra[:, :128]
            spec_refs[nth][IMG_L:, :] = spectra[:, 128:]
        for nth in range(DEEP):
            columns = []
            for look in range(3):
                parts = []
                for part in (0, 1):
                    tiles = [
                        spec_refs[nth][pl.ds(part * IMG_L + info_ref[place + 2 + look], LOOK), :]
                        for place in places[nth]
                    ]
                    parts.append(chosen(tiles).astype(bf16))
                columns.append(jnp.concatenate(parts, axis=0))
            value = dot(u_ref[...], jnp.concatenate(columns, axis=1))
            for look in range(3):
                re = value[:LOOK, look * 128 : look * 128 + 128]
                im = value[LOOK:, look * 128 : look * 128 + 128]
                power = (re * re + im * im).astype(bf16)
                for slot, owner in enumerate(picks[nth]):
                    lanes = slice(slot * HALF, slot * HALF + HALF)
                    if split and look >= NEAR:
                        outs[1][owner, look - NEAR, :, lanes] = power[:, lanes]
                    else:
                        outs[0][owner, look, :, lanes] = power[:, lanes]
        return carry

    lax.fori_loop(0, trips, trip, 0)


def window_table():
    return jnp.asarray(low(np.concatenate(dft_np(IMG_L, -1.0), axis=1)))


def merge_kernel(flag_ref, own_ref, near_ref, far_ref, out_ref):
    lane = lax.broadcasted_iota(jnp.int32, (1, 1, 128), 2)

    def one(owner, carry):
        for part, other_ref in enumerate((near_ref, far_ref)):
            looks = slice(part * NEAR, 3 if part else NEAR)
            taken = 0
            for slot in range(IMG_DEV):
                flag = flag_ref[(owner * IMG_DEV + slot) * 2 + part]
                taken = jnp.where(lane // HALF == slot, flag, taken)
            own = own_ref[owner, looks].astype(f32)
            out_ref[owner, looks] = jnp.where(taken > 0, other_ref[owner].astype(f32), own).astype(bf16)
        return carry

    lax.fori_loop(0, 16, one, 0)


def merged(flags, own, near, far):
    inside = pl.BlockSpec(memory_space=pltpu.VMEM)
    return pl.pallas_call(
        merge_kernel,
        out_shape=jax.ShapeDtypeStruct(own.shape, bf16),
        in_specs=[pl.BlockSpec(memory_space=pltpu.SMEM), inside, inside, inside],
        out_specs=inside,
        compiler_params=pltpu.CompilerParams(vmem_limit_bytes=16 << 20),
    )(flags, own, near, far)


def cross_kernel(info_ref, first_ref, second_ref, w_ref, l_ref, out_ref):
    step = pl.program_id(0)
    lane = lax.broadcasted_iota(jnp.int32, (1, 128), 1)
    for nth in (0, 1):
        slot = 2 * step + nth
        start = info_ref[slot * 2]
        filled = info_ref[slot * 2 + 1] > 0
        rows = []
        for look in range(3):

            def piece(at, half):
                column = start + at
                ref = second_ref if half else first_ref
                source = jnp.where(column < 16, column, column - (8 if look < NEAR else 16))
                return ref[source, look].astype(f32)

            pieces = []
            for part in range(SPAN // 2):
                joined = None
                for spot in range(4):
                    value = piece(2 * part + spot // 2, spot % 2)
                    value = pltpu.roll(value, (HALF * (spot - slot)) % 128, 1)
                    joined = value if spot == 0 else jnp.where(lane < HALF * spot, joined, value)
                pieces.append(joined)
            power = jnp.concatenate(pieces, axis=1)
            mean = jnp.sum(power) * (1.0 / (IMG_C * LOOK))
            rows.append((power * (1.0 / (mean + epsilon)) - 1.0).astype(bf16))
        across = dot(jnp.concatenate(rows, axis=0), w_ref[...]).astype(bf16)
        waves = []
        for look in range(3):
            part = across[look * 128 : look * 128 + 128]
            both = jnp.concatenate([part[:, :IMG_C], part[:, IMG_C:]], axis=0)
            value = dot(l_ref[...], both)
            waves.append((value[:128], value[128:]))
        one_re, one_im = waves[0]
        two_re, two_im = waves[1]
        three_re, three_im = waves[2]
        sum_re = two_re + three_re
        sum_im = two_im + three_im
        total_re = one_re * sum_re + one_im * sum_im + (two_re * three_re + two_im * three_im)
        total_im = one_im * sum_re - one_re * sum_im + (two_im * three_re - two_re * three_im)
        out_ref[nth, 0] = jnp.where(filled, total_re, 0.0).T
        out_ref[nth, 1] = jnp.where(filled, total_im, 0.0).T


def cross(info, first, second):
    whole = lambda shape: pl.BlockSpec(shape, lambda i, s: (0,) * len(shape))
    return pl.pallas_call(
        cross_kernel,
        out_shape=jax.ShapeDtypeStruct((IMG_DEV, 2, IMG_C, LOOK), f32),
        grid_spec=pltpu.PrefetchScalarGridSpec(
            num_scalar_prefetch=1,
            grid=(2,),
            in_specs=[
                pl.BlockSpec(memory_space=pltpu.VMEM),
                pl.BlockSpec(memory_space=pltpu.VMEM),
                whole((IMG_C, 2 * IMG_C)),
                whole((256, 256)),
            ],
            out_specs=pl.BlockSpec((2, 2, IMG_C, LOOK), lambda i, s: (i, 0, 0, 0)),
        ),
        compiler_params=pltpu.CompilerParams(vmem_limit_bytes=40 << 20),
        name="cross",
    )(
        info,
        first,
        second,
        window_table(),
        jnp.asarray(left_form(128, -1.0)),
    )


def strip_facts(anchors, owners, look_bands, strip, count):
    row = lax.dynamic_index_in_dim(owners, strip, 0, keepdims=False)
    facts = jnp.concatenate(
        [
            lax.dynamic_index_in_dim(anchors, strip, 0, keepdims=False),
            lax.dynamic_index_in_dim(look_bands, strip, 0, keepdims=False),
        ],
        axis=1,
    )
    items = jnp.arange(row.shape[0], dtype=jnp.int32)
    earlier = (row[:, None] == row[None, :]) & (items[None, :] < items[:, None])
    rank = jnp.sum(earlier.astype(jnp.int32), axis=1)
    place = row * IMG_DEV + rank
    slots = jnp.arange(count * IMG_DEV, dtype=jnp.int32)
    hot = (place[None, :] == slots[:, None]).astype(jnp.int32)
    filled = jnp.sum(hot, axis=1)
    chosen = jnp.sum(hot[:, :, None] * facts[None], axis=1)
    line = jnp.clip(chosen[:, 0], 0, LINES - IMG_L)
    bands = jnp.clip(chosen[:, 2:], 0, IMG_L - LOOK)
    return line, chosen[:, 1], bands, filled


def reaches(start, filled, column):
    return ((start <= column) & (column < start + SPAN) & (filled > 0)).astype(jnp.int32)


def listed(line, bands, keep):
    pad = jnp.zeros((keep.shape[0], 3), jnp.int32)
    return jnp.concatenate([line[:, None], keep[:, None], bands, pad], axis=1).reshape(-1)


def staged(raw_swath, azimuth_filter, anchors, owners, look_bands):
    count = lax.axis_size("az")
    strips = lax.axis_size("rng")
    strip = lax.axis_index("rng")
    column = lax.axis_index("az")
    line, start, bands, filled = strip_facts(anchors, owners, look_bands, strip, count)
    own = listed(line, bands, reaches(start, filled, column))
    flags = jnp.stack(
        [
            reaches(start, filled, column + SPAN) * (column >= SPAN).astype(jnp.int32),
            reaches(start, filled, column + count),
        ],
        axis=1,
    ).reshape(-1)
    mine = jnp.stack([start, filled], axis=1)
    mine = lax.dynamic_slice_in_dim(mine, column * IMG_DEV, IMG_DEV, 0).reshape(-1)
    line, start, bands, filled = strip_facts(
        anchors, owners, look_bands, jnp.maximum(strip - 1, 0), count
    )
    keep = reaches(start, filled, column + count) * (strip > 0).astype(jnp.int32)
    beyond = listed(line, bands, keep)

    response = azimuth_filter.reshape(COL, 2, AZ_OUTER, AZ_INNER)
    reach = [
        [((r + 1) * count + c, r * count + c + shift) for r in range(strips - 1) for c in range(SPAN - 1)]
        for shift in (SPAN, 0)
    ]
    arrived = []
    chosen = None
    for half in (0, 1):
        if half:
            raw_swath, _ = lax.optimization_barrier((raw_swath, chosen))
        pieces = raw_swath.reshape(count, COL, 2, raw_swath.shape[2])
        chosen = pieces[:, half * HALF : half * HALF + HALF].reshape(count, HALF, 2, 8, 128)
        arrived.append(lax.all_to_all(chosen, "az", split_axis=0, concat_axis=0, tiled=True))
    kept = []
    passed = []
    for half in (0, 1):
        *parts, mine_part = focus(beyond, own, arrived[half], response, half)
        kept.append(mine_part)
        for way in (0, 1):
            passed.append(lax.ppermute(parts[way], ("rng", "az"), reach[way]))
    powers = []
    for half in (0, 1):
        joined = merged(flags, kept[half], *passed[2 * half : 2 * half + 2])
        powers.append(lax.all_to_all(joined, "az", split_axis=0, concat_axis=0, tiled=True))
    return cross(mine, *in_vmem(*powers))[None]


def solution(mesh):
    in_specs = (P("rng", None, "az"), P(("rng", "az"), None, None), P(), P(), P())
    out_specs = P("rng", "az", None, None, None)
    return jax.shard_map(staged, mesh=mesh, in_specs=in_specs, out_specs=out_specs, check_vma=False)
```

```python
import math

import jax
import jax.numpy as jnp
import numpy as np
from jax import lax
from jax.experimental import pallas as pl
from jax.experimental.pallas import tpu as pltpu
from jax.sharding import PartitionSpec as P


AZ_OUTER = 128
AZ_INNER = 128
LINES = 16384
IMG_C = 512
IMG_L = 512
LOOK = 128
COL = 64
IMG_DEV = 4
SPAN = IMG_C // COL
BLOCK = 16
TURN_ROWS = 32
HALF = COL // 2
DEEP = 4
NEAR = 2
epsilon = 1e-06
bf16 = jnp.bfloat16
f32 = jnp.float32


def dft_np(length, sign):
    steps = np.arange(length)
    phase = (steps[:, None] * steps[None, :]) % length
    angle = 2.0 * math.pi * phase / length
    scale = 1.0 / math.sqrt(length)
    return np.cos(angle) * scale, sign * np.sin(angle) * scale


def low(table):
    return np.asarray(table, np.float32).astype(jnp.bfloat16)


def left_form(length, sign):
    re, im = dft_np(length, sign)
    return low(np.block([[re, -im], [im, re]]))


def right_form(length, sign):
    re, im = dft_np(length, sign)
    return low(np.block([[re, im], [-im, re]]))


def twiddles():
    steps = np.arange(AZ_OUTER)
    angle = 2.0 * math.pi * ((steps[:, None] * steps[None, :]) % LINES) / LINES
    return np.stack([np.cos(angle), -np.sin(angle)]).astype(np.float32)


def in_vmem(*values):
    return [pltpu.with_memory_space_constraint(value, pltpu.VMEM) for value in values]


def dot(left, right):
    return jnp.dot(left, right, preferred_element_type=f32)


def focus_kernel(info_ref, *refs, steps, turns):
    arr_ref, filt_ref, l1_ref, t2_ref, t3_ref, l4_ref, tw_ref, w_ref, near_ref, far_ref, kept_ref = refs[:11]
    y_ref, lines_ref, stage_ref, list_ref, *spec_refs = refs[11:]
    step = pl.program_id(0)

    @pl.when(step < steps)
    def _():
        tw_re = tw_ref[0]
        tw_im = tw_ref[1]
        pairs = range(BLOCK // 2)

        def stacked(cell):
            return jnp.concatenate(
                [arr_ref[:, cell, part].reshape(AZ_OUTER, AZ_INNER) for part in (0, 1)], axis=0
            )

        sections = []
        for pair in pairs:
            out = dot(l1_ref[...], jnp.concatenate([stacked(2 * pair), stacked(2 * pair + 1)], axis=1))
            rows = []
            for half in (0, 1):
                re = out[:128, half * 128 : half * 128 + 128]
                im = out[128:, half * 128 : half * 128 + 128]
                rows.append(
                    jnp.concatenate([re * tw_re - im * tw_im, re * tw_im + im * tw_re], axis=1).astype(bf16)
                )
            sections.append(jnp.concatenate(rows, axis=0))
        spectra = []
        for pair in pairs:
            out = dot(sections[pair], t2_ref[...])
            rows = []
            for half in (0, 1):
                re = out[half * 128 : half * 128 + 128, :128]
                im = out[half * 128 : half * 128 + 128, 128:]
                g_re = filt_ref[2 * pair + half, 0].astype(f32)
                g_im = filt_ref[2 * pair + half, 1].astype(f32)
                rows.append(
                    jnp.concatenate([re * g_re - im * g_im, re * g_im + im * g_re], axis=1).astype(bf16)
                )
            spectra.append(jnp.concatenate(rows, axis=0))
        rests = []
        for pair in pairs:
            out = dot(spectra[pair], t3_ref[...])
            columns = []
            for half in (0, 1):
                re = out[half * 128 : half * 128 + 128, :128]
                im = out[half * 128 : half * 128 + 128, 128:]
                columns.append(
                    jnp.concatenate([re * tw_re + im * tw_im, im * tw_re - re * tw_im], axis=0).astype(bf16)
                )
            rests.append(jnp.concatenate(columns, axis=1))
        for pair in pairs:
            out = dot(l4_ref[...], rests[pair])
            for half in (0, 1):
                cell = step * BLOCK + 2 * pair + half
                y_ref[pl.ds(cell * 128, 128), :] = out[:128, half * 128 : half * 128 + 128]
                y_ref[pl.ds((HALF + cell) * 128, 128), :] = out[128:, half * 128 : half * 128 + 128]

    @pl.when(step >= steps)
    def _():
        first = (step - steps) * TURN_ROWS
        for row in range(TURN_ROWS):
            block = y_ref[pl.ds(first + row, 2 * HALF, stride=128), :]
            block = jnp.concatenate([block[:HALF], block[:HALF], block[HALF:], block[HALF:]], axis=0)
            value = block.T.astype(bf16).astype(f32)
            lines_ref[pl.ds(pl.multiple_of((first + row) * 128, 128), 128), :] = value

    @pl.when(step == steps + turns - 1)
    def _():
        look_trips(info_ref, list_ref, lines_ref, stage_ref, spec_refs, w_ref, l4_ref)

        def handed(owner, carry):
            near_ref[owner] = stage_ref[owner, :NEAR]
            far_ref[owner] = stage_ref[owner, NEAR:]
            kept_ref[owner] = stage_ref[16 + owner]
            return carry

        lax.fori_loop(0, 16, handed, 0)


def focus(info, arrived, response, half):
    steps = HALF // BLOCK
    turns = AZ_OUTER // TURN_ROWS
    whole = lambda shape: pl.BlockSpec(shape, lambda i, *s: (0,) * len(shape))
    shapes = [(16, looks, LOOK, 128) for looks in (NEAR, 3 - NEAR, 3)]
    return pl.pallas_call(
        lambda *refs: focus_kernel(*refs, steps=steps, turns=turns),
        out_shape=[jax.ShapeDtypeStruct(shape, bf16) for shape in shapes],
        grid_spec=pltpu.PrefetchScalarGridSpec(
            num_scalar_prefetch=1,
            grid=(steps + turns,),
            in_specs=[
                pl.BlockSpec((16, BLOCK, 2, 8, 128), lambda i, *s: (0, jnp.minimum(i, steps - 1), 0, 0, 0)),
                pl.BlockSpec(
                    (BLOCK, 2, 128, 128), lambda i, *s: (half * steps + jnp.minimum(i, steps - 1), 0, 0, 0)
                ),
                whole((256, 256)),
                whole((256, 256)),
                whole((256, 256)),
                whole((256, 256)),
                whole((2, 128, 128)),
                whole((IMG_L, 2 * IMG_L)),
            ],
            out_specs=[whole(shape) for shape in shapes],
            scratch_shapes=[
                pltpu.VMEM((2 * HALF * 128, 128), f32),
                pltpu.VMEM((LINES, 128), f32),
                pltpu.VMEM((32, 3, LOOK, 128), bf16),
                pltpu.SMEM((2 * 16 * IMG_DEV + 8,), jnp.int32),
            ]
            + [pltpu.VMEM((2 * IMG_L, 128), f32)] * DEEP,
        ),
    )(
        info,
        arrived,
        response,
        jnp.asarray(left_form(128, -1.0)),
        jnp.asarray(right_form(128, -1.0)),
        jnp.asarray(right_form(128, 1.0)),
        jnp.asarray(left_form(128, 1.0)),
        jnp.asarray(twiddles()),
        window_table(),
    )


def look_trips(info_ref, list_ref, lines_ref, stage_ref, spec_refs, w_ref, u_ref):
    lane = lax.broadcasted_iota(jnp.int32, (1, 128), 1)
    low_lanes = lane < 64
    sign = jnp.where(low_lanes, 1.0, -1.0).astype(f32)
    even = lane % 64 < 32
    quarter = lane // HALF
    found = 0
    for entry in range(2 * 16 * IMG_DEV):
        list_ref[found] = entry
        found = found + info_ref[entry * 8 + 1]

    def chosen(tiles):
        return jnp.where(low_lanes, jnp.where(even, tiles[0], tiles[1]), jnp.where(even, tiles[2], tiles[3]))

    def trip(first, deep):
        picks = [
            [list_ref[jnp.minimum(first + nth * 4 + spot, found - 1)] for spot in range(4)]
            for nth in range(deep)
        ]
        for nth in range(deep):
            images = [lines_ref[pl.ds(info_ref[entry * 8], IMG_L), :] for entry in picks[nth]]
            near = jnp.where(even, images[0], images[1])
            far = jnp.where(even, images[2], images[3])
            side = pltpu.roll(jnp.where(low_lanes, far, near), 64, 1) * sign
            main = jnp.where(low_lanes, near, far).astype(bf16)
            right = jnp.concatenate(
                [
                    jnp.concatenate([main, side.astype(bf16)], axis=1),
                    jnp.concatenate([(-side).astype(bf16), main], axis=1),
                ],
                axis=0,
            )
            spectra = dot(w_ref[...], right)
            spec_refs[nth][:IMG_L, :] = spectra[:, :128]
            spec_refs[nth][IMG_L:, :] = spectra[:, 128:]
        for nth in range(deep):
            columns = []
            for look in range(3):
                parts = []
                for part in (0, 1):
                    tiles = [
                        spec_refs[nth][pl.ds(part * IMG_L + info_ref[entry * 8 + 2 + look], LOOK), :]
                        for entry in picks[nth]
                    ]
                    parts.append(chosen(tiles).astype(bf16))
                columns.append(jnp.concatenate(parts, axis=0))
            value = dot(u_ref[...], jnp.concatenate(columns, axis=1))
            for look in range(3):
                re = value[:LOOK, look * 128 : look * 128 + 128]
                im = value[LOOK:, look * 128 : look * 128 + 128]
                power = re * re + im * im
                for spot, entry in enumerate(picks[nth]):
                    slot = entry % IMG_DEV
                    placed = pltpu.roll(power, (HALF * (slot - spot + IMG_DEV)) % 128, 1).astype(bf16)
                    row = entry // IMG_DEV
                    stage_ref[row, look] = jnp.where(quarter == slot, placed, stage_ref[row, look])

    def wide(at, carry):
        trip(at * 4 * DEEP, DEEP)
        return carry

    def narrow(at, carry):
        trip(most * 4 * DEEP, DEEP // 2)
        return carry

    most = (found + 2 * DEEP - 1) // (4 * DEEP)
    lax.fori_loop(0, most, wide, 0)
    lax.fori_loop(0, (found > most * 4 * DEEP).astype(jnp.int32), narrow, 0)


def window_table():
    return jnp.asarray(low(np.concatenate(dft_np(IMG_L, -1.0), axis=1)))


def merge_kernel(flag_ref, own_ref, near_ref, far_ref, out_ref):
    lane = lax.broadcasted_iota(jnp.int32, (1, 1, 128), 2)

    def one(owner, carry):
        for part, other_ref in enumerate((near_ref, far_ref)):
            looks = slice(part * NEAR, 3 if part else NEAR)
            taken = 0
            for slot in range(IMG_DEV):
                flag = flag_ref[(owner * IMG_DEV + slot) * 2 + part]
                taken = jnp.where(lane // HALF == slot, flag, taken)
            own = own_ref[owner, looks].astype(f32)
            out_ref[owner, looks] = jnp.where(taken > 0, other_ref[owner].astype(f32), own).astype(bf16)
        return carry

    lax.fori_loop(0, 16, one, 0)


def merged(flags, own, near, far):
    inside = pl.BlockSpec(memory_space=pltpu.VMEM)
    return pl.pallas_call(
        merge_kernel,
        out_shape=jax.ShapeDtypeStruct(own.shape, bf16),
        in_specs=[pl.BlockSpec(memory_space=pltpu.SMEM), inside, inside, inside],
        out_specs=inside,
        compiler_params=pltpu.CompilerParams(vmem_limit_bytes=16 << 20),
    )(flags, own, near, far)


def cross_kernel(info_ref, first_ref, second_ref, w_ref, l_ref, out_ref):
    step = pl.program_id(0)
    lane = lax.broadcasted_iota(jnp.int32, (1, 128), 1)
    for nth in (0, 1):
        slot = 2 * step + nth
        start = info_ref[slot * 2]
        filled = info_ref[slot * 2 + 1] > 0
        rows = []
        for look in range(3):

            def piece(at, half):
                column = start + at
                ref = second_ref if half else first_ref
                source = jnp.where(column < 16, column, column - (8 if look < NEAR else 16))
                return ref[source, look].astype(f32)

            pieces = []
            for part in range(SPAN // 2):
                joined = None
                for spot in range(4):
                    value = piece(2 * part + spot // 2, spot % 2)
                    value = pltpu.roll(value, (HALF * (spot - slot)) % 128, 1)
                    joined = value if spot == 0 else jnp.where(lane < HALF * spot, joined, value)
                pieces.append(joined)
            power = jnp.concatenate(pieces, axis=1)
            mean = jnp.sum(power) * (1.0 / (IMG_C * LOOK))
            rows.append((power * (1.0 / (mean + epsilon)) - 1.0).astype(bf16))
        across = dot(jnp.concatenate(rows, axis=0), w_ref[...]).astype(bf16)
        waves = []
        for look in range(3):
            part = across[look * 128 : look * 128 + 128]
            both = jnp.concatenate([part[:, :IMG_C], part[:, IMG_C:]], axis=0)
            value = dot(l_ref[...], both)
            waves.append((value[:128], value[128:]))
        one_re, one_im = waves[0]
        two_re, two_im = waves[1]
        three_re, three_im = waves[2]
        sum_re = two_re + three_re
        sum_im = two_im + three_im
        total_re = one_re * sum_re + one_im * sum_im + (two_re * three_re + two_im * three_im)
        total_im = one_im * sum_re - one_re * sum_im + (two_im * three_re - two_re * three_im)
        out_ref[nth, 0] = jnp.where(filled, total_re, 0.0).T
        out_ref[nth, 1] = jnp.where(filled, total_im, 0.0).T


def cross(info, first, second):
    whole = lambda shape: pl.BlockSpec(shape, lambda i, s: (0,) * len(shape))
    return pl.pallas_call(
        cross_kernel,
        out_shape=jax.ShapeDtypeStruct((IMG_DEV, 2, IMG_C, LOOK), f32),
        grid_spec=pltpu.PrefetchScalarGridSpec(
            num_scalar_prefetch=1,
            grid=(2,),
            in_specs=[
                pl.BlockSpec(memory_space=pltpu.VMEM),
                pl.BlockSpec(memory_space=pltpu.VMEM),
                whole((IMG_C, 2 * IMG_C)),
                whole((256, 256)),
            ],
            out_specs=pl.BlockSpec((2, 2, IMG_C, LOOK), lambda i, s: (i, 0, 0, 0)),
        ),
        compiler_params=pltpu.CompilerParams(vmem_limit_bytes=40 << 20),
        name="cross",
    )(
        info,
        first,
        second,
        window_table(),
        jnp.asarray(left_form(128, -1.0)),
    )


def strip_facts(anchors, owners, look_bands, strip, count):
    row = lax.dynamic_index_in_dim(owners, strip, 0, keepdims=False)
    facts = jnp.concatenate(
        [
            lax.dynamic_index_in_dim(anchors, strip, 0, keepdims=False),
            lax.dynamic_index_in_dim(look_bands, strip, 0, keepdims=False),
        ],
        axis=1,
    )
    items = jnp.arange(row.shape[0], dtype=jnp.int32)
    earlier = (row[:, None] == row[None, :]) & (items[None, :] < items[:, None])
    rank = jnp.sum(earlier.astype(jnp.int32), axis=1)
    place = row * IMG_DEV + rank
    slots = jnp.arange(count * IMG_DEV, dtype=jnp.int32)
    hot = (place[None, :] == slots[:, None]).astype(jnp.int32)
    filled = jnp.sum(hot, axis=1)
    chosen = jnp.sum(hot[:, :, None] * facts[None], axis=1)
    line = jnp.clip(chosen[:, 0], 0, LINES - IMG_L)
    bands = jnp.clip(chosen[:, 2:], 0, IMG_L - LOOK)
    return line, chosen[:, 1], bands, filled


def reaches(start, filled, column):
    return ((start <= column) & (column < start + SPAN) & (filled > 0)).astype(jnp.int32)


def listed(line, bands, keep):
    pad = jnp.zeros((keep.shape[0], 3), jnp.int32)
    return jnp.concatenate([line[:, None], keep[:, None], bands, pad], axis=1).reshape(-1)


def staged(raw_swath, azimuth_filter, anchors, owners, look_bands):
    count = lax.axis_size("az")
    strips = lax.axis_size("rng")
    strip = lax.axis_index("rng")
    column = lax.axis_index("az")
    line, start, bands, filled = strip_facts(anchors, owners, look_bands, strip, count)
    own = listed(line, bands, reaches(start, filled, column))
    flags = jnp.stack(
        [
            reaches(start, filled, column + SPAN) * (column >= SPAN).astype(jnp.int32),
            reaches(start, filled, column + count),
        ],
        axis=1,
    ).reshape(-1)
    mine = jnp.stack([start, filled], axis=1)
    mine = lax.dynamic_slice_in_dim(mine, column * IMG_DEV, IMG_DEV, 0).reshape(-1)
    line, start, bands, filled = strip_facts(
        anchors, owners, look_bands, jnp.maximum(strip - 1, 0), count
    )
    keep = reaches(start, filled, column + count) * (strip > 0).astype(jnp.int32)
    info = jnp.concatenate([listed(line, bands, keep), own])

    response = azimuth_filter.reshape(COL, 2, AZ_OUTER, AZ_INNER)
    reach = [
        [((r + 1) * count + c, r * count + c + shift) for r in range(strips - 1) for c in range(SPAN - 1)]
        for shift in (SPAN, 0)
    ]
    arrived = []
    chosen = None
    for half in (0, 1):
        if half:
            raw_swath, _ = lax.optimization_barrier((raw_swath, chosen))
        pieces = raw_swath.reshape(count, COL, 2, raw_swath.shape[2])
        chosen = pieces[:, half * HALF : half * HALF + HALF].reshape(count, HALF, 2, 8, 128)
        arrived.append(lax.all_to_all(chosen, "az", split_axis=0, concat_axis=0, tiled=True))
    kept = []
    passed = []
    for half in (0, 1):
        *parts, mine_part = focus(info, arrived[half], response, half)
        kept.append(mine_part)
        for way in (0, 1):
            passed.append(lax.ppermute(parts[way], ("rng", "az"), reach[way]))
    powers = []
    for half in (0, 1):
        joined = merged(flags, kept[half], *passed[2 * half : 2 * half + 2])
        powers.append(lax.all_to_all(joined, "az", split_axis=0, concat_axis=0, tiled=True))
    return cross(mine, *in_vmem(*powers))[None]


def solution(mesh):
    in_specs = (P("rng", None, "az"), P(("rng", "az"), None, None), P(), P(), P())
    out_specs = P("rng", "az", None, None, None)
    return jax.shard_map(staged, mesh=mesh, in_specs=in_specs, out_specs=out_specs, check_vma=False)
```
